32 devices in a mesh: gx: 4 (over x, core), gy: 8 (over z, y).
Axes of the slice: x: 2, y: 2, z: 4, core: 2. Of those that a mesh axis runs over, the one named last changes fastest.
Arguments:
- increment: float32 [8, 2048, 1024], P(None, 'gx', 'gy'), may hold values from -6 to 6
- deviation: float32 [8, 2048, 1024], P(None, 'gx', 'gy'), may hold values from 0.5 to 2
- land_sea: int32 [8, 2048, 1024], P(None, 'gx', 'gy'), may hold values 0 or 1
- filter_steps: int32 [8], replicated, may hold values from 1 to 2, as said below
- zonal_rate: float32 [8], replicated, may hold values from 0.0009765625 to 0.03
- meridional_rate: float32 [8], replicated, may hold values from 0.001953125 to 0.03
Outputs:
- covaried: float32 [8, 2048, 1024], P(None, 'gx', 'gy')
The draws below stay inside these ranges and needn't reach their ends.
Inputs may be any that keep to these rules, and one draw needn't show every extreme that they name: `filter_steps`: some level has 2 repetitions and some level has 1.
All inputs are finite; a program needn't handle non-finite values. No bound on the sum of `land_sea` on one device may be relied on, other than what follows from the above.
Results may differ from the reference program's by a relative error of at most 0.0003.
Values sent between devices are 32-bit elements; how exact they have to be, the bound alone decides.
A program may use at most 128 MiB of HBM per device.

```python
import math
import jax
import jax.numpy as jnp
from jax import lax

L = 8
MAXSTEPS = 2
NX = 2048
NY = 1024


def draw_filter_steps(key, part):
    values = jax.random.randint(jax.random.fold_in(key, 11), (L,), 1, MAXSTEPS + 1)
    shuffled = jax.random.permutation(jax.random.fold_in(key, 12), L)
    values = values.at[shuffled[0]].set(MAXSTEPS)
    values = values.at[shuffled[1]].set(1)
    return values.astype(jnp.int32)


def place_ends(drawn, own_key, least, largest):
    longest = drawn.shape.index(max(drawn.shape))
    spots = []
    for shift in (0, 1):
        where = [jax.random.randint(jax.random.fold_in(own_key, axis), (), 0, length) for axis, length in enumerate(drawn.shape)]
        where[longest] = (where[longest] + shift) % drawn.shape[longest]
        spots.append(tuple(where))
    return drawn.at[spots[0]].set(least).at[spots[1]].set(largest)


def level_of(key, extent, shards, low, largest):
    factor_of, own = 1.0, jax.random.fold_in(key, 6)
    for axis_at, blocks in shards:
        steps = jnp.exp(jax.random.uniform(jax.random.fold_in(own, axis_at), (blocks,), jnp.float32, low / len(shards), largest / len(shards)))
        factor_of = factor_of * jnp.repeat(steps, extent[axis_at] // blocks).reshape([-1 if axis == axis_at else 1 for axis in range(len(extent))])
    return factor_of


def gaussian(key, dims, spread, limit, cuts=(), dtype=jnp.bfloat16):
    array = jax.random.normal(key, dims, jnp.float32) * spread
    if len(cuts) > 0:
        array = level_of(key, dims, cuts, -0.22, 0.18) * array
    return jnp.clip(array, min=-limit, max=limit).astype(dtype)


def setup_inputs(seed: int = 0) -> dict:
    streams_of = jax.random.split(jax.random.key(seed), 7)
    increment = gaussian(streams_of[0], (L, NX, NY), 1.0, 6.0, ((1, 4), (2, 8)), jnp.float32)
    deviation = jnp.clip(jnp.exp(math.log(2.0) - 1.3862944 * jax.random.uniform(streams_of[1], (L, NX, NY), jnp.float32) ** level_of(streams_of[1], (L, NX, NY), ((1, 4), (2, 8)), -0.2, 0.2)), 0.5, 2.0)
    land_sea = place_ends((jax.random.randint(streams_of[2], (L, NX, NY), 0, 4) < 3).astype(jnp.int32), jax.random.fold_in(streams_of[2], 1), 0, 1)
    filter_steps = draw_filter_steps(jax.random.fold_in(streams_of[6], 71), 0)
    zonal_rate = jnp.clip(jnp.exp(jax.random.uniform(streams_of[4], (L,), jnp.float32, math.log(0.0009765625), math.log(0.03))), 0.0009765625, 0.03)
    meridional_rate = jnp.clip(jnp.exp(jax.random.uniform(streams_of[5], (L,), jnp.float32, math.log(0.001953125), math.log(0.03))), 0.001953125, 0.03)
    return dict(increment=increment, deviation=deviation, land_sea=land_sea, filter_steps=filter_steps, zonal_rate=zonal_rate, meridional_rate=meridional_rate)


gain_base = 3.0 ** 0.125


def section_gain(decay_rate, filter_steps):
    fading = -jnp.expm1(-decay_rate)
    return gain_base * fading ** (1.0 - 1.0 / (16.0 * filter_steps.astype(jnp.float32)))


def recursive_pass(field, decay_rate, section_weight, direction, backward):
    ordered = jnp.moveaxis(field, direction, 0)
    if backward:
        ordered = ordered[::-1]
    factor = jnp.exp(-decay_rate)[:, None]
    weight = section_weight[:, None]

    def advance(carried, column):
        section_one = factor * carried[0] + weight * column
        section_two = factor * carried[1] + weight * section_one
        section_three = factor * carried[2] + weight * section_two
        section_four = factor * carried[3] + weight * section_three
        return (section_one, section_two, section_three, section_four), section_four

    empty_state = jnp.zeros(ordered.shape[1:], jnp.float32)
    _, result = lax.scan(advance, (empty_state, empty_state, empty_state, empty_state), ordered)
    if backward:
        result = result[::-1]
    return jnp.moveaxis(result, 0, direction)


def reference(increment, deviation, land_sea, filter_steps, zonal_rate, meridional_rate):
    wetness = land_sea.astype(jnp.float32)
    field = deviation * wetness * increment
    for repeat in range(MAXSTEPS):
        active = (filter_steps > repeat)[:, None, None]
        current = field
        for direction, rates in ((1, zonal_rate), (2, meridional_rate)):
            weights = section_gain(rates, filter_steps)
            current = wetness * recursive_pass(current, rates, weights, direction, False)
            current = wetness * recursive_pass(current, rates, weights, direction, True)
        field = jnp.where(active, current, field)
    return deviation * field
```

```python
import functools

import jax
import jax.numpy as jnp
from jax import lax
from jax.experimental import pallas as pl
from jax.experimental.pallas import tpu as pltpu
from jax.sharding import PartitionSpec as P

BX = 256
MAXSTEPS = 2
UNROLL = 2
gain_base = 3.0**0.125
MESH = pl.DeviceIdType.MESH
f32, bf16 = jnp.float32, jnp.bfloat16


def section_gain(decay_rate, filter_steps):
    fading = -jnp.expm1(-decay_rate)
    return gain_base * fading ** (1.0 - 1.0 / (16.0 * filter_steps.astype(f32)))


def halves(table):
    high = lax.reduce_precision(table, 8, 7)
    return high.astype(bf16), (table - high).astype(bf16)


def binomials(count):
    return (
        jnp.ones_like(count),
        count,
        count * (count + 1.0) / 2.0,
        count * (count + 1.0) * (count + 2.0) / 6.0,
    )


def powers(weight):
    return (jnp.ones_like(weight), weight, weight * weight, weight * weight * weight)


def tile_table(rate, weight, size, backward):
    places = jnp.arange(size).astype(f32)
    lagged = places[:, None] - places[None, :]
    if backward:
        lagged = -lagged
    span = jnp.maximum(lagged, 0.0)
    w = weight[:, None, None]
    return jnp.where(
        lagged > -0.5,
        (w * w * w * w) * jnp.exp(-rate[:, None, None] * span) * ((span + 1.0) * (span + 2.0) * (span + 3.0) / 6.0),
        0.0,
    )


def end_tables(rate, weight, size, backward):
    places = jnp.arange(size).astype(f32)
    if backward:
        places = size - 1.0 - places
    remain, ahead = size - places, places + 1.0
    a, w = rate[:, None], weight[:, None]
    pw = powers(w)
    fin = jnp.stack(
        [w * pw[k] * jnp.exp(-a * (remain - 1.0)) * b for k, b in enumerate(binomials(remain[None]))], 1
    )
    res = jnp.stack(
        [pw[3 - k] * jnp.exp(-a * ahead) * binomials(ahead[None])[3 - k] for k in range(4)], 1
    )
    return fin, res


def pad4(rows):
    return jnp.pad(rows, ((0, 0), (0, 4), (0, 0)))


def stacked_ends(fin, res):
    fin_hi, fin_lo = halves(pad4(fin))
    res_hi, res_lo = halves(pad4(res))
    return (
        jnp.concatenate([fin_hi, fin_lo], 1),
        jnp.concatenate([res_hi, res_hi, res_lo, jnp.zeros_like(res_lo)], 1),
    )


def step_coefs(rate, weight, spans):
    pw = powers(weight)
    out = []
    for span in spans:
        count = jnp.full_like(rate, float(span))
        fall = jnp.exp(-rate * count)
        for k, b in enumerate(binomials(count)):
            out.append(fall * pw[k] * b)
    return jnp.stack(out, 1)


def split(value):
    high = value.astype(bf16)
    return high, (value - high.astype(f32)).astype(bf16)


def kernel(
    nx, ny, levels, rows, cols,
    coef_x, coef_y, active,
    inc, dev, sea, txh, txl, fx, rx, wy, fy, ry,
    out,
    field, inside, closing_x, end_x, got_x, end_y, got_y, pass_y, chain_y, carry_y,
    sx_sem, rx_sem, sp_sem, rp_sem, sc_sem, rc_sem,
):
    gx, gy = lax.axis_index("gx"), lax.axis_index("gy")
    nb = rows // BX
    row4 = lax.broadcasted_iota(jnp.int32, (8, 128), 0) < 4
    half = ny // 2
    inner, outer = lax.rem(gy, 2), gy // 2
    partner = gy + 1 - 2 * inner

    def advance(state, coef, l, index):
        total = coef[l, 4 * index] * state
        for j in range(1, 4):
            total += coef[l, 4 * index + j] * pltpu.roll(state, j, 0)
        keep = jnp.concatenate([row4] * (state.shape[1] // 128), 1)
        return jnp.where(keep, total, 0.0)

    def three(state):
        high = state.astype(bf16).astype(f32)
        return jnp.concatenate([high, state - high, high, jnp.zeros_like(high)], 0).astype(bf16)

    def dot(a, b, ca=1, cb=0):
        return lax.dot_general(a, b, (((ca,), (cb,)), ((), ())), preferred_element_type=f32)

    def x_copy(l, stage, d, backward):
        target = gx - d if backward else gx + d
        return pltpu.make_async_remote_copy(
            src_ref=end_x.at[stage, l],
            dst_ref=got_x.at[stage, l, d - 1],
            send_sem=sx_sem.at[stage, l, d - 1],
            recv_sem=rx_sem.at[stage, l, d - 1],
            device_id=(target, gy),
            device_id_type=MESH,
        )

    def p_copy(l, stage):
        return pltpu.make_async_remote_copy(
            src_ref=end_y.at[stage, l],
            dst_ref=got_y.at[stage, l],
            send_sem=sp_sem.at[stage, l],
            recv_sem=rp_sem.at[stage, l],
            device_id=(gx, partner),
            device_id_type=MESH,
        )

    def c_copy(l, stage, backward):
        return pltpu.make_async_remote_copy(
            src_ref=pass_y.at[stage, l],
            dst_ref=chain_y.at[stage, l],
            send_sem=sc_sem.at[stage, l],
            recv_sem=rc_sem.at[stage, l],
            device_id=(gx, gy - 2 if backward else gy + 2),
            device_id_type=MESH,
        )

    def x_sends(d, backward):
        return gx >= d if backward else gx + d < nx

    def x_gets(d, backward):
        return gx + d < nx if backward else gx >= d

    def c_sends(backward):
        return outer > 0 if backward else outer < half - 1

    def c_gets(backward):
        return outer < half - 1 if backward else outer > 0

    def start_x(l, value, rep, backward):
        back = int(backward)
        stage = 2 * rep + back
        wide = jnp.concatenate([value[b * BX:(b + 1) * BX] for b in range(nb)], 1)
        high, low = split(wide)
        both = dot(fx[back, l], high) + dot(fx[back, l], low)
        closing = both[:8] + both[8:]
        closing_x[l] = closing
        order = range(nb - 1, -1, -1) if backward else range(nb)
        end = None
        for b in order:
            piece = closing[:, b * cols:(b + 1) * cols]
            end = piece if end is None else advance(end, coef_x, l, 0) + piece
        end_x[stage, l] = end
        for d in range(1, nx):
            @pl.when(x_sends(d, backward))
            def _():
                x_copy(l, stage, d, backward).start()
        th = txh[back, l]
        inside[l] = dot(th, high) + dot(th, low) + dot(txl[back, l], high)

    def fin_x(l, rep, backward):
        back = int(backward)
        stage = 2 * rep + back
        for d in range(1, nx):
            @pl.when(x_gets(d, backward))
            def _():
                x_copy(l, stage, d, backward).wait_recv()
        carry = got_x[stage, l, 0]
        for d in range(2, nx):
            carry += advance(got_x[stage, l, d - 1], coef_x, l, d - 1)
        order = list(range(nb - 1, -1, -1) if backward else range(nb))
        starts = [None] * nb
        for n, b in enumerate(order):
            starts[b] = carry
            if n < nb - 1:
                carry = advance(carry, coef_x, l, 0) + closing_x[l, :, b * cols:(b + 1) * cols]
        wide = inside[l] + dot(rx[back, l], three(jnp.concatenate(starts, 1)), 0, 0)
        value = jnp.concatenate([wide[:, b * cols:(b + 1) * cols] for b in range(nb)], 0)
        return value * sea[l].astype(f32)

    def start_y(l, value, rep, backward):
        back = int(backward)
        stage = 2 * rep + back
        high, low = split(value)
        pair = jnp.concatenate([high, low], 1)
        ends = jnp.concatenate([fy[back, l]] * 2, 1)
        both = dot(ends, pair, 1, 1)
        end_y[stage, l] = both[:8] + both[8:]
        p_copy(l, stage).start()
        wide = dot(pair, wy[back, l])
        field[l] = wide[:, :cols] + wide[:, cols:]

    def relay_y(l, rep, backward):
        back = int(backward)
        stage = 2 * rep + back
        p_copy(l, stage).wait_recv()
        own, other = end_y[stage, l], got_y[stage, l]
        is_first = inner == (1 if backward else 0)
        first = jnp.where(is_first, own, other)
        second = jnp.where(is_first, other, own)
        joint = advance(first, coef_y, l, 0) + second

        @pl.when(c_gets(backward))
        def _():
            c_copy(l, stage, backward).wait_recv()

        come = chain_y[stage, l]
        pass_y[stage, l] = advance(come, coef_y, l, 1) + joint

        @pl.when(c_sends(backward))
        def _():
            c_copy(l, stage, backward).start()

        carry_y[l] = jnp.where(is_first, come, advance(come, coef_y, l, 0) + other)

    def fin_y(l, rep, backward):
        back = int(backward)
        value = field[l] + dot(three(carry_y[l]), ry[back, l], 0, 0)
        return value * sea[l].astype(f32)

    def each(body):
        lax.fori_loop(0, levels, lambda l, c: (body(l), c)[1], 0, unroll=UNROLL)

    got_x[...] = jnp.zeros_like(got_x)
    chain_y[...] = jnp.zeros_like(chain_y)
    barrier = pltpu.get_barrier_semaphore()
    for d in range(1, nx):
        pl.semaphore_signal(barrier, inc=1, device_id=(lax.rem(gx + d, nx), gy), device_id_type=MESH)
    pl.semaphore_signal(barrier, inc=1, device_id=(gx, partner), device_id_type=MESH)

    @pl.when(outer > 0)
    def _():
        pl.semaphore_signal(barrier, inc=1, device_id=(gx, gy - 2), device_id_type=MESH)

    @pl.when(outer < half - 1)
    def _():
        pl.semaphore_signal(barrier, inc=1, device_id=(gx, gy + 2), device_id_type=MESH)

    pl.semaphore_wait(barrier, nx + jnp.minimum(outer, 1) + jnp.minimum(half - 1 - outer, 1))

    def begin(l):
        value = dev[l] * sea[l].astype(f32) * inc[l]
        out[l] = jnp.zeros_like(value)
        start_x(l, value, 0, False)

    each(begin)

    def finish(l, rep):
        value = fin_y(l, rep, True)
        share = active[l, rep]
        out[l] = share * (dev[l] * value) + (1.0 - share) * out[l]
        return value

    def repetition(rep, c):
        each(lambda l: start_x(l, fin_x(l, rep, False), rep, True))
        each(lambda l: start_y(l, fin_x(l, rep, True), rep, False))
        each(lambda l: relay_y(l, rep, False))
        each(lambda l: start_y(l, fin_y(l, rep, False), rep, True))
        each(lambda l: relay_y(l, rep, True))

        @pl.when(rep < MAXSTEPS - 1)
        def _():
            each(lambda l: start_x(l, finish(l, rep), rep + 1, False))

        @pl.when(rep == MAXSTEPS - 1)
        def _():
            each(lambda l: (finish(l, rep), None)[1])

        return c

    lax.fori_loop(0, MAXSTEPS, repetition, 0)

    def drain(l):
        for rep in range(MAXSTEPS):
            for backward in (False, True):
                stage = 2 * rep + int(backward)
                for d in range(1, nx):
                    @pl.when(x_sends(d, backward))
                    def _():
                        x_copy(l, stage, d, backward).wait_send()
                p_copy(l, stage).wait_send()

                @pl.when(c_sends(backward))
                def _():
                    c_copy(l, stage, backward).wait_send()

    lax.fori_loop(0, levels, lambda l, c: (drain(l), c)[1], 0)


def on_device(nx, ny, increment, deviation, land_sea, filter_steps, zonal_rate, meridional_rate):
    levels, rows, cols = increment.shape
    nb = rows // BX
    wx = section_gain(zonal_rate, filter_steps)
    wm = section_gain(meridional_rate, filter_steps)
    txh, txl, fx, rx, wy, fy, ry = [], [], [], [], [], [], []
    for backward in (False, True):
        high, low = halves(tile_table(zonal_rate, wx, BX, backward))
        txh.append(high)
        txl.append(low)
        fin, res = stacked_ends(*end_tables(zonal_rate, wx, BX, backward))
        fx.append(fin)
        rx.append(res)
        high, low = halves(tile_table(meridional_rate, wm, cols, not backward))
        wy.append(
            jnp.concatenate(
                [jnp.concatenate([high, low], 2), jnp.concatenate([high, jnp.zeros_like(low)], 2)], 1
            )
        )
        fin, res = stacked_ends(*end_tables(meridional_rate, wm, cols, backward))
        fy.append(fin)
        ry.append(res)
    tables = [jnp.stack(t) for t in (txh, txl, fx, rx, wy, fy, ry)]
    coef_x = step_coefs(zonal_rate, wx, [BX] + [rows * d for d in range(1, nx - 1)])
    coef_y = step_coefs(meridional_rate, wm, [cols, 2 * cols])
    active = (filter_steps[:, None] > jnp.arange(MAXSTEPS)[None]).astype(f32)
    smem = pl.BlockSpec(memory_space=pltpu.SMEM)
    vmem = pl.BlockSpec(memory_space=pltpu.VMEM)
    stages = 2 * MAXSTEPS
    dma = pltpu.SemaphoreType.DMA
    return pl.pallas_call(
        functools.partial(kernel, nx, ny, levels, rows, cols),
        out_shape=jax.ShapeDtypeStruct(increment.shape, f32),
        in_specs=[smem] * 3 + [vmem] * 10,
        out_specs=vmem,
        scratch_shapes=[
            pltpu.VMEM((levels, rows, cols), f32),
            pltpu.VMEM((levels, BX, nb * cols), f32),
            pltpu.VMEM((levels, 8, nb * cols), f32),
            pltpu.VMEM((stages, levels, 8, cols), f32),
            pltpu.VMEM((stages, levels, nx - 1, 8, cols), f32),
            pltpu.VMEM((stages, levels, 8, rows), f32),
            pltpu.VMEM((stages, levels, 8, rows), f32),
            pltpu.VMEM((stages, levels, 8, rows), f32),
            pltpu.VMEM((stages, levels, 8, rows), f32),
            pltpu.VMEM((levels, 8, rows), f32),
            dma((stages, levels, nx - 1)),
            dma((stages, levels, nx - 1)),
            dma((stages, levels)),
            dma((stages, levels)),
            dma((stages, levels)),
            dma((stages, levels)),
        ],
        compiler_params=pltpu.CompilerParams(
            collective_id=0, has_side_effects=True, vmem_limit_bytes=60 * 1024 * 1024
        ),
    )(coef_x, coef_y, active, increment, deviation, land_sea, *tables)


def solution(mesh):
    placed = (P(None, "gx", "gy"), P(None, "gx", "gy"), P(None, "gx", "gy"), P(), P(), P())
    body = functools.partial(on_device, mesh.shape["gx"], mesh.shape["gy"])
    return jax.shard_map(
        body, mesh=mesh, in_specs=placed, out_specs=P(None, "gx", "gy"), check_vma=False
    )
```

```python
import functools

import jax
import jax.numpy as jnp
from jax import lax
from jax.experimental import pallas as pl
from jax.experimental.pallas import tpu as pltpu
from jax.sharding import PartitionSpec as P

BX = 256
MAXSTEPS = 2
UNROLL = 2
gain_base = 3.0**0.125
MESH = pl.DeviceIdType.MESH
f32, bf16 = jnp.float32, jnp.bfloat16


def section_gain(decay_rate, filter_steps):
    fading = -jnp.expm1(-decay_rate)
    return gain_base * fading ** (1.0 - 1.0 / (16.0 * filter_steps.astype(f32)))


def binomials(count):
    return (
        jnp.ones_like(count),
        count,
        count * (count + 1.0) / 2.0,
        count * (count + 1.0) * (count + 2.0) / 6.0,
    )


def by_row(values, row):
    total = jnp.zeros(row.shape, f32)
    for k, value in enumerate(values):
        total = jnp.where(row == k, value, total)
    return total


def split(value):
    high = value.astype(bf16)
    return high, (value - high.astype(f32)).astype(bf16)


def kernel(
    nx, ny, levels, rows, cols,
    steps, rate_x, rate_y, gains,
    inc, dev, sea,
    out,
    txh, txl, fx, rx, wy, fy, ry, coef_x, coef_y,
    field, inside, closing_x, end_x, got_x, end_y, got_y, pass_y, chain_y, carry_y,
    sx_sem, rx_sem, sp_sem, rp_sem, sc_sem, rc_sem,
):
    gx, gy = lax.axis_index("gx"), lax.axis_index("gy")
    nb = rows // BX
    half = ny // 2
    inner, outer = lax.rem(gy, 2), gy // 2
    partner = gy + 1 - 2 * inner

    def advance(state, coef, l, index):
        copies = state.shape[1] // 128
        total = None
        for j in range(4):
            scale = jnp.concatenate([coef[l, 4 * index + j]] * copies, 1)
            term = scale * (pltpu.roll(state, j, 0) if j else state)
            total = term if total is None else total + term
        return total

    def three(state):
        high = state.astype(bf16).astype(f32)
        return jnp.concatenate([high, state - high, high, jnp.zeros_like(high)], 0).astype(bf16)

    def dot(a, b, ca=1, cb=0):
        return lax.dot_general(a, b, (((ca,), (cb,)), ((), ())), preferred_element_type=f32)

    def x_copy(l, stage, d, backward):
        target = gx - d if backward else gx + d
        return pltpu.make_async_remote_copy(
            src_ref=end_x.at[stage, l],
            dst_ref=got_x.at[stage, l, d - 1],
            send_sem=sx_sem.at[stage, l, d - 1],
            recv_sem=rx_sem.at[stage, l, d - 1],
            device_id=(target, gy),
            device_id_type=MESH,
        )

    def p_copy(l, stage):
        return pltpu.make_async_remote_copy(
            src_ref=end_y.at[stage, l],
            dst_ref=got_y.at[stage, l],
            send_sem=sp_sem.at[stage, l],
            recv_sem=rp_sem.at[stage, l],
            device_id=(gx, partner),
            device_id_type=MESH,
        )

    def c_copy(l, stage, backward):
        return pltpu.make_async_remote_copy(
            src_ref=pass_y.at[stage, l],
            dst_ref=chain_y.at[stage, l],
            send_sem=sc_sem.at[stage, l],
            recv_sem=rc_sem.at[stage, l],
            device_id=(gx, gy - 2 if backward else gy + 2),
            device_id_type=MESH,
        )

    def x_sends(d, backward):
        return gx >= d if backward else gx + d < nx

    def x_gets(d, backward):
        return gx + d < nx if backward else gx >= d

    def c_sends(backward):
        return outer > 0 if backward else outer < half - 1

    def c_gets(backward):
        return outer < half - 1 if backward else outer > 0

    def start_x(l, value, rep, backward):
        back = int(backward)
        stage = 2 * rep + back
        wide = jnp.concatenate([value[b * BX:(b + 1) * BX] for b in range(nb)], 1)
        high, low = split(wide)
        both = dot(fx[back, l], high) + dot(fx[back, l], low)
        closing = both[:8] + both[8:]
        closing_x[l] = closing
        order = range(nb - 1, -1, -1) if backward else range(nb)
        end = None
        for b in order:
            piece = closing[:, b * cols:(b + 1) * cols]
            end = piece if end is None else advance(end, coef_x, l, 0) + piece
        end_x[stage, l] = end
        for d in range(1, nx):
            @pl.when(x_sends(d, backward))
            def _():
                x_copy(l, stage, d, backward).start()
        th = txh[back, l]
        inside[l] = dot(th, high) + dot(th, low) + dot(txl[back, l], high)

    def fin_x(l, rep, backward):
        back = int(backward)
        stage = 2 * rep + back
        for d in range(1, nx):
            @pl.when(x_gets(d, backward))
            def _():
                x_copy(l, stage, d, backward).wait_recv()
        carry = got_x[stage, l, 0]
        for d in range(2, nx):
            carry += advance(got_x[stage, l, d - 1], coef_x, l, d - 1)
        order = list(range(nb - 1, -1, -1) if backward else range(nb))
        starts = [None] * nb
        for n, b in enumerate(order):
            starts[b] = carry
            if n < nb - 1:
                carry = advance(carry, coef_x, l, 0) + closing_x[l, :, b * cols:(b + 1) * cols]
        wide = inside[l] + dot(rx[back, l], three(jnp.concatenate(starts, 1)), 0, 0)
        value = jnp.concatenate([wide[:, b * cols:(b + 1) * cols] for b in range(nb)], 0)
        return value * sea[l].astype(f32)

    def start_y(l, value, rep, backward):
        back = int(backward)
        stage = 2 * rep + back
        high, low = split(value)
        pair = jnp.concatenate([high, low], 1)
        ends = jnp.concatenate([fy[back, l]] * 2, 1)
        both = dot(ends, pair, 1, 1)
        end_y[stage, l] = both[:8] + both[8:]
        p_copy(l, stage).start()
        wide = dot(pair, wy[back, l])
        field[l] = wide[:, :cols] + wide[:, cols:]

    def relay_y(l, rep, backward):
        back = int(backward)
        stage = 2 * rep + back
        p_copy(l, stage).wait_recv()
        own, other = end_y[stage, l], got_y[stage, l]
        is_first = inner == (1 if backward else 0)
        first = jnp.where(is_first, own, other)
        second = jnp.where(is_first, other, own)
        joint = advance(first, coef_y, l, 0) + second

        @pl.when(c_gets(backward))
        def _():
            c_copy(l, stage, backward).wait_recv()

        come = chain_y[stage, l]
        pass_y[stage, l] = advance(come, coef_y, l, 1) + joint

        @pl.when(c_sends(backward))
        def _():
            c_copy(l, stage, backward).start()

        carry_y[l] = jnp.where(is_first, come, advance(come, coef_y, l, 0) + other)

    def fin_y(l, rep, backward):
        back = int(backward)
        value = field[l] + dot(three(carry_y[l]), ry[back, l], 0, 0)
        return value * sea[l].astype(f32)

    def each(body):
        lax.fori_loop(0, levels, lambda l, c: (body(l), c)[1], 0, unroll=UNROLL)

    side = 128
    lags = (
        lax.broadcasted_iota(jnp.int32, (side, side), 0) - lax.broadcasted_iota(jnp.int32, (side, side), 1)
    ).astype(f32)

    def shape_of(lag):
        span = jnp.maximum(lag, 0.0)
        return span, jnp.where(lag > -0.5, (span + 1.0) * (span + 2.0) * (span + 3.0) / 6.0, 0.0)

    near = (shape_of(lags), shape_of(-lags))
    far = (shape_of(side + lags), shape_of(side - lags))

    def tile(shape, rate, weight4):
        return split(weight4 * shape[1] * jnp.exp(-rate * shape[0]))

    def ends(fin, res, l, size, rate, weight):
        row = lax.broadcasted_iota(jnp.int32, (8, size), 0)
        lane = lax.broadcasted_iota(jnp.int32, (8, size), 1).astype(f32)
        pw = [jnp.full((8, size), v) for v in (1.0, weight, weight * weight, weight * weight * weight)]
        for back in (0, 1):
            places = size - 1.0 - lane if back else lane
            remain, ahead = size - places, places + 1.0
            leave, come = binomials(remain), binomials(ahead)
            final = by_row([weight * pw[k] * leave[k] for k in range(4)], row) * jnp.exp(-rate * (remain - 1.0))
            high = final.astype(bf16).astype(f32)
            fin[back, l] = jnp.concatenate([high, final - high], 0).astype(bf16)
            answer = by_row([pw[3 - k] * come[3 - k] for k in range(4)], row) * jnp.exp(-rate * ahead)
            high = answer.astype(bf16).astype(f32)
            res[back, l] = jnp.concatenate(
                [high, high, answer - high, jnp.zeros_like(high)], 0
            ).astype(bf16)

    def coefs(coef, l, spans, rate, weight):
        row = lax.broadcasted_iota(jnp.int32, (8, 128), 0)
        power = (1.0, weight, weight * weight, weight * weight * weight)
        for n, span in enumerate(spans):
            fall = jnp.where(row < 4, jnp.exp(jnp.full((8, 128), -rate * span)), 0.0)
            count = (1.0, span, span * (span + 1.0) / 2.0, span * (span + 1.0) * (span + 2.0) / 6.0)
            for j in range(4):
                coef[l, 4 * n + j] = fall * (power[j] * count[j])

    def build(l):
        rate, weight = rate_x[l], gains[0, l]
        weight4 = weight * weight * weight * weight
        zero = jnp.zeros((side, side), bf16)
        lower, upper = pl.ds(0, side), pl.ds(side, side)
        for back in (0, 1):
            one, two = tile(near[back], rate, weight4), tile(far[back], rate, weight4)
            for ref, close, distant in ((txh, one[0], two[0]), (txl, one[1], two[1])):
                ref[back, l, lower, lower] = close
                ref[back, l, upper, upper] = close
                ref[back, l, lower, upper] = distant if back else zero
                ref[back, l, upper, lower] = zero if back else distant
        ends(fx, rx, l, BX, rate, weight)
        coefs(coef_x, l, [float(BX)] + [float(rows * d) for d in range(1, nx - 1)], rate, weight)
        rate, weight = rate_y[l], gains[1, l]
        weight4 = weight * weight * weight * weight
        for back in (0, 1):
            high, low = tile(near[1 - back], rate, weight4)
            wy[back, l, lower, lower] = high
            wy[back, l, upper, lower] = high
            wy[back, l, lower, upper] = low
            wy[back, l, upper, upper] = zero
        ends(fy, ry, l, cols, rate, weight)
        coefs(coef_y, l, [float(cols), 2.0 * cols], rate, weight)

    got_x[...] = jnp.zeros_like(got_x)
    chain_y[...] = jnp.zeros_like(chain_y)
    barrier = pltpu.get_barrier_semaphore()
    for d in range(1, nx):
        pl.semaphore_signal(barrier, inc=1, device_id=(lax.rem(gx + d, nx), gy), device_id_type=MESH)
    pl.semaphore_signal(barrier, inc=1, device_id=(gx, partner), device_id_type=MESH)

    @pl.when(outer > 0)
    def _():
        pl.semaphore_signal(barrier, inc=1, device_id=(gx, gy - 2), device_id_type=MESH)

    @pl.when(outer < half - 1)
    def _():
        pl.semaphore_signal(barrier, inc=1, device_id=(gx, gy + 2), device_id_type=MESH)

    lax.fori_loop(0, levels, lambda l, c: (build(l), c)[1], 0)
    pl.semaphore_wait(barrier, nx + jnp.minimum(outer, 1) + jnp.minimum(half - 1 - outer, 1))

    def begin(l):
        value = dev[l] * sea[l].astype(f32) * inc[l]
        out[l] = jnp.zeros_like(value)
        start_x(l, value, 0, False)

    each(begin)

    def finish(l, rep):
        value = fin_y(l, rep, True)
        share = jnp.clip((steps[l] - rep).astype(f32), 0.0, 1.0)
        out[l] = share * (dev[l] * value) + (1.0 - share) * out[l]
        return value

    def repetition(rep, c):
        each(lambda l: start_x(l, fin_x(l, rep, False), rep, True))
        each(lambda l: start_y(l, fin_x(l, rep, True), rep, False))
        each(lambda l: relay_y(l, rep, False))
        each(lambda l: start_y(l, fin_y(l, rep, False), rep, True))
        each(lambda l: relay_y(l, rep, True))

        @pl.when(rep < MAXSTEPS - 1)
        def _():
            each(lambda l: start_x(l, finish(l, rep), rep + 1, False))

        @pl.when(rep == MAXSTEPS - 1)
        def _():
            each(lambda l: (finish(l, rep), None)[1])

        return c

    lax.fori_loop(0, MAXSTEPS, repetition, 0)

    def drain(l):
        for rep in range(MAXSTEPS):
            for backward in (False, True):
                stage = 2 * rep + int(backward)
                for d in range(1, nx):
                    @pl.when(x_sends(d, backward))
                    def _():
                        x_copy(l, stage, d, backward).wait_send()
                p_copy(l, stage).wait_send()

                @pl.when(c_sends(backward))
                def _():
                    c_copy(l, stage, backward).wait_send()

    lax.fori_loop(0, levels, lambda l, c: (drain(l), c)[1], 0)


def on_device(nx, ny, increment, deviation, land_sea, filter_steps, zonal_rate, meridional_rate):
    levels, rows, cols = increment.shape
    nb = rows // BX
    gains = section_gain(jnp.stack([zonal_rate, meridional_rate]), filter_steps[None])
    smem = pl.BlockSpec(memory_space=pltpu.SMEM)
    vmem = pl.BlockSpec(memory_space=pltpu.VMEM)
    stages = 2 * MAXSTEPS
    dma = pltpu.SemaphoreType.DMA
    return pl.pallas_call(
        functools.partial(kernel, nx, ny, levels, rows, cols),
        out_shape=jax.ShapeDtypeStruct(increment.shape, f32),
        in_specs=[smem] * 4 + [vmem] * 3,
        out_specs=vmem,
        scratch_shapes=[
            pltpu.VMEM((2, levels, BX, BX), bf16),
            pltpu.VMEM((2, levels, BX, BX), bf16),
            pltpu.VMEM((2, levels, 16, BX), bf16),
            pltpu.VMEM((2, levels, 32, BX), bf16),
            pltpu.VMEM((2, levels, 2 * cols, 2 * cols), bf16),
            pltpu.VMEM((2, levels, 16, cols), bf16),
            pltpu.VMEM((2, levels, 32, cols), bf16),
            pltpu.VMEM((levels, 4 * (nx - 1), 8, 128), f32),
            pltpu.VMEM((levels, 8, 8, 128), f32),
            pltpu.VMEM((levels, rows, cols), f32),
            pltpu.VMEM((levels, BX, nb * cols), f32),
            pltpu.VMEM((levels, 8, nb * cols), f32),
            pltpu.VMEM((stages, levels, 8, cols), f32),
            pltpu.VMEM((stages, levels, nx - 1, 8, cols), f32),
            pltpu.VMEM((stages, levels, 8, rows), f32),
            pltpu.VMEM((stages, levels, 8, rows), f32),
            pltpu.VMEM((stages, levels, 8, rows), f32),
            pltpu.VMEM((stages, levels, 8, rows), f32),
            pltpu.VMEM((levels, 8, rows), f32),
            dma((stages, levels, nx - 1)),
            dma((stages, levels, nx - 1)),
            dma((stages, levels)),
            dma((stages, levels)),
            dma((stages, levels)),
            dma((stages, levels)),
        ],
        compiler_params=pltpu.CompilerParams(
            collective_id=0, has_side_effects=True, vmem_limit_bytes=40 * 1024 * 1024
        ),
    )(filter_steps, zonal_rate, meridional_rate, gains, increment, deviation, land_sea)


def solution(mesh):
    placed = (P(None, "gx", "gy"), P(None, "gx", "gy"), P(None, "gx", "gy"), P(), P(), P())
    body = functools.partial(on_device, mesh.shape["gx"], mesh.shape["gy"])
    return jax.shard_map(
        body, mesh=mesh, in_specs=placed, out_specs=P(None, "gx", "gy"), check_vma=False
    )
```

```python
import functools

import jax
import jax.numpy as jnp
from jax import lax
from jax.experimental import pallas as pl
from jax.experimental.pallas import tpu as pltpu
from jax.sharding import PartitionSpec as P

BX = 256
MAXSTEPS = 2
UNROLL = 2
gain_base = 3.0**0.125
MESH = pl.DeviceIdType.MESH
f32, bf16 = jnp.float32, jnp.bfloat16


def section_gain(decay_rate, filter_steps):
    fading = -jnp.expm1(-decay_rate)
    return gain_base * fading ** (1.0 - 1.0 / (16.0 * filter_steps.astype(f32)))


def binomials(count):
    return (
        jnp.ones_like(count),
        count,
        count * (count + 1.0) / 2.0,
        count * (count + 1.0) * (count + 2.0) / 6.0,
    )


def by_row(values, row):
    total = jnp.zeros(row.shape, f32)
    for k, value in enumerate(values):
        total = jnp.where(row == k, value, total)
    return total


def split(value):
    high = value.astype(bf16)
    return high, (value - high.astype(f32)).astype(bf16)


def kernel(
    nx, ny, levels, rows, cols,
    steps, rate_x, rate_y, gains,
    inc_hbm, dev_hbm, sea_hbm,
    out,
    txh, txl, fx, rx, wy, fy, ry, coef_x, coef_y,
    field, inside, closing_x, end_x, got_x, end_y, got_y, pass_y, chain_y, dev, sea,
    sx_sem, rx_sem, sp_sem, rp_sem, sc_sem, rc_sem, in_sem,
):
    gx, gy = lax.axis_index("gx"), lax.axis_index("gy")
    nb = rows // BX
    half = ny // 2
    inner, outer = lax.rem(gy, 2), gy // 2
    partner = gy + 1 - 2 * inner

    def advance(state, coef, l, index):
        copies = state.shape[1] // 128
        total = None
        for j in range(4):
            scale = jnp.concatenate([coef[l, 4 * index + j]] * copies, 1)
            term = scale * (pltpu.roll(state, j, 0) if j else state)
            total = term if total is None else total + term
        return total

    def three(state):
        high = state.astype(bf16).astype(f32)
        return jnp.concatenate([high, state - high, high, jnp.zeros_like(high)], 0).astype(bf16)

    def dot(a, b, ca=1, cb=0):
        return lax.dot_general(a, b, (((ca,), (cb,)), ((), ())), preferred_element_type=f32)

    def x_copy(l, stage, d, backward):
        target = gx - d if backward else gx + d
        return pltpu.make_async_remote_copy(
            src_ref=end_x.at[stage, l, pl.ds(0, 4)],
            dst_ref=got_x.at[stage, l, d - 1, pl.ds(0, 4)],
            send_sem=sx_sem.at[stage, l, d - 1],
            recv_sem=rx_sem.at[stage, l, d - 1],
            device_id=(target, gy),
            device_id_type=MESH,
        )

    def p_copy(l, stage):
        return pltpu.make_async_remote_copy(
            src_ref=end_y.at[stage, l, pl.ds(0, 4)],
            dst_ref=got_y.at[stage, l, pl.ds(0, 4)],
            send_sem=sp_sem.at[stage, l],
            recv_sem=rp_sem.at[stage, l],
            device_id=(gx, partner),
            device_id_type=MESH,
        )

    def c_copy(l, stage, d, backward):
        target = gy - 2 * d if backward else gy + 2 * d
        return pltpu.make_async_remote_copy(
            src_ref=pass_y.at[stage, l, pl.ds(0, 4)],
            dst_ref=chain_y.at[stage, l, d - 1, pl.ds(0, 4)],
            send_sem=sc_sem.at[stage, l, d - 1],
            recv_sem=rc_sem.at[stage, l, d - 1],
            device_id=(gx, target),
            device_id_type=MESH,
        )

    def x_sends(d, backward):
        return gx >= d if backward else gx + d < nx

    def x_gets(d, backward):
        return gx + d < nx if backward else gx >= d

    def c_sends(d, backward):
        return outer >= d if backward else outer + d < half

    def c_gets(d, backward):
        return outer + d < half if backward else outer >= d

    def start_x(l, value, rep, backward):
        back = int(backward)
        stage = 2 * rep + back
        wide = jnp.concatenate([value[b * BX:(b + 1) * BX] for b in range(nb)], 1)
        high, low = split(wide)
        both = dot(fx[back, l], high) + dot(fx[back, l], low)
        closing = both[:8] + both[8:]
        closing_x[l] = closing
        order = range(nb - 1, -1, -1) if backward else range(nb)
        end = None
        for b in order:
            piece = closing[:, b * cols:(b + 1) * cols]
            end = piece if end is None else advance(end, coef_x, l, 0) + piece
        end_x[stage, l] = end
        for d in range(1, nx):
            @pl.when(x_sends(d, backward))
            def _():
                x_copy(l, stage, d, backward).start()
        for b in range(nb):
            field[l, b * BX:(b + 1) * BX] = value[b * BX:(b + 1) * BX]

    def middle_x(l, backward):
        back = int(backward)
        wide = jnp.concatenate([field[l, b * BX:(b + 1) * BX] for b in range(nb)], 1)
        high, low = split(wide)
        th = txh[back, l]
        inside[l] = dot(th, high) + dot(th, low) + dot(txl[back, l], high)

    def fin_x(l, rep, backward):
        back = int(backward)
        stage = 2 * rep + back
        for d in range(1, nx):
            @pl.when(x_gets(d, backward))
            def _():
                x_copy(l, stage, d, backward).wait_recv()
        carry = got_x[stage, l, 0]
        for d in range(2, nx):
            carry += advance(got_x[stage, l, d - 1], coef_x, l, d - 1)
        order = list(range(nb - 1, -1, -1) if backward else range(nb))
        starts = [None] * nb
        for n, b in enumerate(order):
            starts[b] = carry
            if n < nb - 1:
                carry = advance(carry, coef_x, l, 0) + closing_x[l, :, b * cols:(b + 1) * cols]
        wide = inside[l] + dot(rx[back, l], three(jnp.concatenate(starts, 1)), 0, 0)
        value = jnp.concatenate([wide[:, b * cols:(b + 1) * cols] for b in range(nb)], 0)
        return value * sea[l].astype(f32)

    def start_y(l, value, rep, backward):
        back = int(backward)
        stage = 2 * rep + back
        high, low = split(value)
        pair = jnp.concatenate([high, low], 1)
        ends = jnp.concatenate([fy[back, l]] * 2, 1)
        both = dot(ends, pair, 1, 1)
        end_y[stage, l] = both[:8] + both[8:]
        p_copy(l, stage).start()
        field[l] = value

    def middle_y(l, backward):
        back = int(backward)
        pair = jnp.concatenate(split(field[l]), 1)
        wide = dot(pair, wy[back, l])
        field[l] = wide[:, :cols] + wide[:, cols:]

    def relay_y(l, rep, backward):
        back = int(backward)
        stage = 2 * rep + back
        p_copy(l, stage).wait_recv()
        own, other = end_y[stage, l], got_y[stage, l]
        is_first = inner == (1 if backward else 0)
        first = jnp.where(is_first, own, other)
        second = jnp.where(is_first, other, own)
        pass_y[stage, l] = advance(first, coef_y, l, 0) + second
        for d in range(1, half):
            @pl.when(c_sends(d, backward))
            def _():
                c_copy(l, stage, d, backward).start()

    def fin_y(l, rep, backward):
        back = int(backward)
        stage = 2 * rep + back
        for d in range(1, half):
            @pl.when(c_gets(d, backward))
            def _():
                c_copy(l, stage, d, backward).wait_recv()
        come = chain_y[stage, l, 0]
        for d in range(2, half):
            come += advance(chain_y[stage, l, d - 1], coef_y, l, d - 1)
        is_first = inner == (1 if backward else 0)
        carry = jnp.where(is_first, come, advance(come, coef_y, l, 0) + got_y[stage, l])
        value = field[l] + dot(three(carry), ry[back, l], 0, 0)
        return value * sea[l].astype(f32)

    def each(body):
        lax.fori_loop(0, levels, lambda l, c: (body(l), c)[1], 0, unroll=UNROLL)

    incoming = [
        pltpu.make_async_copy(src, dst, in_sem.at[n])
        for n, (src, dst) in enumerate(((inc_hbm, field), (dev_hbm, dev), (sea_hbm, sea)))
    ]
    for copy in incoming:
        copy.start()
    side = 128
    lags = (
        lax.broadcasted_iota(jnp.int32, (side, side), 0) - lax.broadcasted_iota(jnp.int32, (side, side), 1)
    ).astype(f32)

    def shape_of(lag):
        span = jnp.maximum(lag, 0.0)
        return span, jnp.where(lag > -0.5, (span + 1.0) * (span + 2.0) * (span + 3.0) / 6.0, 0.0)

    near = (shape_of(lags), shape_of(-lags))
    far = (shape_of(side + lags), shape_of(side - lags))

    def tile(shape, rate, weight4):
        return split(weight4 * shape[1] * jnp.exp(-rate * shape[0]))

    def ends(fin, res, l, size, rate, weight):
        row = lax.broadcasted_iota(jnp.int32, (8, size), 0)
        lane = lax.broadcasted_iota(jnp.int32, (8, size), 1).astype(f32)
        pw = [jnp.full((8, size), v) for v in (1.0, weight, weight * weight, weight * weight * weight)]
        for back in (0, 1):
            places = size - 1.0 - lane if back else lane
            remain, ahead = size - places, places + 1.0
            leave, come = binomials(remain), binomials(ahead)
            final = by_row([weight * pw[k] * leave[k] for k in range(4)], row) * jnp.exp(-rate * (remain - 1.0))
            high = final.astype(bf16).astype(f32)
            fin[back, l] = jnp.concatenate([high, final - high], 0).astype(bf16)
            answer = by_row([pw[3 - k] * come[3 - k] for k in range(4)], row) * jnp.exp(-rate * ahead)
            high = answer.astype(bf16).astype(f32)
            res[back, l] = jnp.concatenate(
                [high, high, answer - high, jnp.zeros_like(high)], 0
            ).astype(bf16)

    def coefs(coef, l, spans, rate, weight):
        row = lax.broadcasted_iota(jnp.int32, (8, 128), 0)
        power = (1.0, weight, weight * weight, weight * weight * weight)
        for n, span in enumerate(spans):
            fall = jnp.where(row < 4, jnp.exp(jnp.full((8, 128), -rate * span)), 0.0)
            count = (1.0, span, span * (span + 1.0) / 2.0, span * (span + 1.0) * (span + 2.0) / 6.0)
            for j in range(4):
                coef[l, 4 * n + j] = fall * (power[j] * count[j])

    def build(l):
        rate, weight = rate_x[l], gains[0, l]
        weight4 = weight * weight * weight * weight
        zero = jnp.zeros((side, side), bf16)
        lower, upper = pl.ds(0, side), pl.ds(side, side)
        for back in (0, 1):
            one, two = tile(near[back], rate, weight4), tile(far[back], rate, weight4)
            for ref, close, distant in ((txh, one[0], two[0]), (txl, one[1], two[1])):
                ref[back, l, lower, lower] = close
                ref[back, l, upper, upper] = close
                ref[back, l, lower, upper] = distant if back else zero
                ref[back, l, upper, lower] = zero if back else distant
        ends(fx, rx, l, BX, rate, weight)
        coefs(coef_x, l, [float(BX)] + [float(rows * d) for d in range(1, nx - 1)], rate, weight)
        rate, weight = rate_y[l], gains[1, l]
        weight4 = weight * weight * weight * weight
        for back in (0, 1):
            high, low = tile(near[1 - back], rate, weight4)
            wy[back, l, lower, lower] = high
            wy[back, l, upper, lower] = high
            wy[back, l, lower, upper] = low
            wy[back, l, upper, upper] = zero
        ends(fy, ry, l, cols, rate, weight)
        coefs(coef_y, l, [float(cols)] + [2.0 * cols * d for d in range(1, half - 1)], rate, weight)

    got_x[...] = jnp.zeros_like(got_x)
    got_y[...] = jnp.zeros_like(got_y)
    chain_y[...] = jnp.zeros_like(chain_y)
    barrier = pltpu.get_barrier_semaphore()
    for d in range(1, nx):
        pl.semaphore_signal(barrier, inc=1, device_id=(lax.rem(gx + d, nx), gy), device_id_type=MESH)
    pl.semaphore_signal(barrier, inc=1, device_id=(gx, partner), device_id_type=MESH)
    for d in range(1, half):
        pl.semaphore_signal(barrier, inc=1, device_id=(gx, lax.rem(gy + 2 * d, ny)), device_id_type=MESH)
    lax.fori_loop(0, levels, lambda l, c: (build(l), c)[1], 0)
    pl.semaphore_wait(barrier, nx + half - 1)

    for copy in incoming:
        copy.wait()

    def begin(l):
        value = dev[l] * sea[l].astype(f32) * field[l]
        out[l] = jnp.zeros_like(value)
        start_x(l, value, 0, False)

    each(begin)

    def finish(l, rep):
        value = fin_y(l, rep, True)
        share = jnp.clip((steps[l] - rep).astype(f32), 0.0, 1.0)
        out[l] = share * (dev[l] * value) + (1.0 - share) * out[l]
        return value

    def repetition(rep, c):
        def pairs(l, backward):
            relay_y(l, rep, backward)
            middle_y(l, backward)

        each(lambda l: middle_x(l, False))
        each(lambda l: start_x(l, fin_x(l, rep, False), rep, True))
        each(lambda l: middle_x(l, True))
        each(lambda l: start_y(l, fin_x(l, rep, True), rep, False))
        each(lambda l: pairs(l, False))
        each(lambda l: start_y(l, fin_y(l, rep, False), rep, True))
        each(lambda l: pairs(l, True))

        @pl.when(rep < MAXSTEPS - 1)
        def _():
            each(lambda l: start_x(l, finish(l, rep), rep + 1, False))

        @pl.when(rep == MAXSTEPS - 1)
        def _():
            each(lambda l: (finish(l, rep), None)[1])

        return c

    lax.fori_loop(0, MAXSTEPS, repetition, 0)

    def drain(l):
        for rep in range(MAXSTEPS):
            for backward in (False, True):
                stage = 2 * rep + int(backward)
                for d in range(1, nx):
                    @pl.when(x_sends(d, backward))
                    def _():
                        x_copy(l, stage, d, backward).wait_send()
                p_copy(l, stage).wait_send()

                for d in range(1, half):
                    @pl.when(c_sends(d, backward))
                    def _():
                        c_copy(l, stage, d, backward).wait_send()

    lax.fori_loop(0, levels, lambda l, c: (drain(l), c)[1], 0)


def on_device(nx, ny, increment, deviation, land_sea, filter_steps, zonal_rate, meridional_rate):
    levels, rows, cols = increment.shape
    nb = rows // BX
    gains = section_gain(jnp.stack([zonal_rate, meridional_rate]), filter_steps[None])
    smem = pl.BlockSpec(memory_space=pltpu.SMEM)
    hbm = pl.BlockSpec(memory_space=pltpu.HBM)
    vmem = pl.BlockSpec(memory_space=pltpu.VMEM)
    stages = 2 * MAXSTEPS
    dma = pltpu.SemaphoreType.DMA
    return pl.pallas_call(
        functools.partial(kernel, nx, ny, levels, rows, cols),
        out_shape=jax.ShapeDtypeStruct(increment.shape, f32),
        in_specs=[smem] * 4 + [hbm] * 3,
        out_specs=vmem,
        scratch_shapes=[
            pltpu.VMEM((2, levels, BX, BX), bf16),
            pltpu.VMEM((2, levels, BX, BX), bf16),
            pltpu.VMEM((2, levels, 16, BX), bf16),
            pltpu.VMEM((2, levels, 32, BX), bf16),
            pltpu.VMEM((2, levels, 2 * cols, 2 * cols), bf16),
            pltpu.VMEM((2, levels, 16, cols), bf16),
            pltpu.VMEM((2, levels, 32, cols), bf16),
            pltpu.VMEM((levels, 4 * (nx - 1), 8, 128), f32),
            pltpu.VMEM((levels, 4 * (ny // 2 - 1), 8, 128), f32),
            pltpu.VMEM((levels, rows, cols), f32),
            pltpu.VMEM((levels, BX, nb * cols), f32),
            pltpu.VMEM((levels, 8, nb * cols), f32),
            pltpu.VMEM((stages, levels, 8, cols), f32),
            pltpu.VMEM((stages, levels, nx - 1, 8, cols), f32),
            pltpu.VMEM((stages, levels, 8, rows), f32),
            pltpu.VMEM((stages, levels, 8, rows), f32),
            pltpu.VMEM((stages, levels, 8, rows), f32),
            pltpu.VMEM((stages, levels, ny // 2 - 1, 8, rows), f32),
            pltpu.VMEM((levels, rows, cols), f32),
            pltpu.VMEM((levels, rows, cols), jnp.int32),
            dma((stages, levels, nx - 1)),
            dma((stages, levels, nx - 1)),
            dma((stages, levels)),
            dma((stages, levels)),
            dma((stages, levels, ny // 2 - 1)),
            dma((stages, levels, ny // 2 - 1)),
            dma((3,)),
        ],
        compiler_params=pltpu.CompilerParams(
            collective_id=0, has_side_effects=True, vmem_limit_bytes=40 * 1024 * 1024
        ),
    )(filter_steps, zonal_rate, meridional_rate, gains, increment, deviation, land_sea)


def solution(mesh):
    placed = (P(None, "gx", "gy"), P(None, "gx", "gy"), P(None, "gx", "gy"), P(), P(), P())
    body = functools.partial(on_device, mesh.shape["gx"], mesh.shape["gy"])
    return jax.shard_map(
        body, mesh=mesh, in_specs=placed, out_specs=P(None, "gx", "gy"), check_vma=False
    )
```
